256 devices in a mesh: strata: 16 (over z_lo, x), users: 16 (over y, z_hi, core).
Axes of the slice: x: 4, y: 4, z: 8 (z_hi: 2, z_lo: 4; z = z_hi * 4 + z_lo), core: 2. Of those that a mesh axis runs over, the one named last changes fastest.
Arguments:
- user_factors: float32 [524288, 256], P(('strata', 'users')), may hold values from -1.5 to 1.5
- item_factors: float32 [16384, 256], P(('strata', 'users')), may hold values from -1.5 to 1.5
- tile_rows: int32 [16, 16, 2, 64], P('strata', 'users'), may hold values from 0 to 15, as said below
- tile_columns: int32 [16, 16, 2, 64], P('strata', 'users'), may hold values from 0 to 7, as said below
- tile_counts: int32 [16, 16, 2], P('strata', 'users'), may hold values from 8 to 64, as said below
- ratings: int32 [16, 16, 2, 64, 128, 128], P('strata', 'users'), may hold values from 0 to 5
Outputs:
- updated_users: float32 [524288, 256], P(('strata', 'users'))
- updated_items: float32 [16384, 256], P(('strata', 'users'))
The draws below stay inside these ranges and needn't reach their ends.
Inputs may be any that keep to these rules, and one draw needn't show every extreme that they name: `tile_rows`: row tile of each slot within the device's users. `tile_columns`: item tile of each slot within the step's item block; a device's slots of one step name distinct pairs of user tile and item tile, padding slots included. `tile_counts`: in every step some device uses all 64 slots.
All inputs are finite; a program needn't handle non-finite values.
Results may differ from the reference program's by a relative error of at most 0.0004.
Values may be sent and summed in bfloat16 or wider, within the bound.
A program may use at most 128 MiB of HBM per device.

```python
import jax
import jax.numpy as jnp
from jax import lax

K = 256
TILE = 128
ITEM_TILES = 8
ROW_TILES = 16
MAXT = 64
STEPS = 2
STRATA = 16
SHARDS = 16
USERS_ALL = 524288
ITEMS = 16384


def tile_lists(key):
    key = jax.random.fold_in(key, 7)
    keys = jax.random.split(key, STRATA * SHARDS * STEPS)
    cells = ROW_TILES * ITEM_TILES
    picks = jax.vmap(lambda single: jax.random.permutation(single, cells)[:MAXT])(keys)
    picks = picks.reshape(STRATA, SHARDS, STEPS, MAXT).astype(jnp.int32)
    return (picks // ITEM_TILES, picks % ITEM_TILES)


def draw_tile_rows(key, part):
    return tile_lists(key)[0]


def draw_tile_columns(key, part):
    return tile_lists(key)[1]


def draw_tile_counts(key, part):
    lowest = max(MAXT // 8, 1)
    spread = MAXT - lowest
    first_key, second_key, third_key = jax.random.split(jax.random.fold_in(key, 11), 3)
    first = jax.random.randint(first_key, (STRATA, SHARDS, STEPS), 0, spread + 1)
    second = jax.random.randint(second_key, (STRATA, SHARDS, STEPS), 0, spread + 1)
    counts = lowest + first * second // max(spread, 1)
    chosen = jax.random.randint(third_key, (STEPS,), 0, STRATA * SHARDS)
    fullest = (jnp.arange(STRATA * SHARDS)[:, None] == chosen[None, :]).reshape(STRATA, SHARDS, STEPS)
    return jnp.where(fullest, MAXT, counts).astype(jnp.int32)


def draw_ratings(key, part):
    first_key, second_key = jax.random.split(jax.random.fold_in(key, 13))
    density = jax.random.randint(first_key, (STRATA, SHARDS, STEPS, MAXT, 1, 1), 10, 61)
    raw = jax.random.randint(second_key, (STRATA, SHARDS, STEPS, MAXT, TILE, TILE), 0, 500)
    return jnp.where(raw % 100 < density, raw // 100 + 1, 0).astype(jnp.int32)


def steps_of(stream_key, extent, pieces, low, largest):
    factor_of = 1.0
    for position, blocks in pieces:
        draws = jax.random.uniform(jax.random.fold_in(jax.random.fold_in(stream_key, 6), position), (blocks,), jnp.float32, low / len(pieces), largest / len(pieces))
        factor_of = factor_of * jnp.repeat(jnp.exp(draws), extent[position] // blocks).reshape((-1,) + (1,) * (len(extent) - 1 - position))
    return factor_of


def centred(rng, dims, deviation, bound, cuts=(), held_as=jnp.bfloat16):
    gain = steps_of(rng, dims, cuts, -0.22, 0.18) if cuts else 1.0
    values = jax.random.normal(rng, dims, jnp.float32) * deviation * gain
    return jnp.minimum(jnp.maximum(values, -bound), bound).astype(held_as)


def setup_inputs(seed: int = 0) -> dict:
    key_of = jax.random.split(jax.random.key(seed), 7)
    user_factors = centred(key_of[0], (USERS_ALL, K), 0.25, 1.5, ((0, 256),), jnp.float32)
    item_factors = centred(key_of[1], (ITEMS, K), 0.25, 1.5, ((0, 256),), jnp.float32)
    tile_rows = draw_tile_rows(jax.random.fold_in(key_of[6], 71), 0)
    tile_columns = draw_tile_columns(jax.random.fold_in(key_of[6], 71), 0)
    tile_counts = draw_tile_counts(jax.random.fold_in(key_of[6], 71), 0)
    ratings = draw_ratings(jax.random.fold_in(key_of[6], 71), 0)
    return dict(user_factors=user_factors, item_factors=item_factors, tile_rows=tile_rows, tile_columns=tile_columns, tile_counts=tile_counts, ratings=ratings)


def shard_terms(user_low, block_low, row_blocks, column_blocks, count, rating_tiles):
    user_tiles = user_low[row_blocks].astype(jnp.float32)
    item_tiles = block_low[column_blocks].astype(jnp.float32)
    predicted = jnp.einsum('mik,mjk->mij', user_tiles, item_tiles)
    in_list = jnp.arange(MAXT) < count
    observed = (rating_tiles > 0) & in_list[:, None, None]
    residual = jnp.where(observed, rating_tiles.astype(jnp.float32) - predicted, 0.0).astype(jnp.bfloat16)
    residual = lax.optimization_barrier(residual).astype(jnp.float32)
    user_terms = jnp.einsum('mij,mjk->mik', residual, item_tiles)
    item_terms = jnp.einsum('mij,mik->mjk', residual, user_tiles)
    user_grad = jnp.zeros((ROW_TILES, TILE, K), jnp.float32).at[row_blocks].add(user_terms)
    item_grad = jnp.zeros((ITEM_TILES, TILE, K), jnp.float32).at[column_blocks].add(item_terms)
    return user_grad, item_grad


def stratum_terms(inputs):
    user_low, block_low, row_blocks, column_blocks, counts, rating_tiles = inputs
    user_grad, item_grad = jax.vmap(shard_terms, in_axes=(0, None, 0, 0, 0, 0))(
        user_low, block_low, row_blocks, column_blocks, counts, rating_tiles)
    return user_grad, jnp.sum(item_grad, axis=0)


def reference(user_factors, item_factors, tile_rows, tile_columns, tile_counts, ratings):
    users_now = user_factors
    items_now = item_factors
    for step_index in range(STEPS):
        user_low = users_now.astype(jnp.bfloat16).reshape(STRATA, SHARDS, ROW_TILES, TILE, K)
        item_low = items_now.astype(jnp.bfloat16).reshape(STRATA, ITEM_TILES, TILE, K)
        block_now = jnp.roll(item_low, step_index, axis=0)
        user_grad, item_grad = lax.map(stratum_terms, (
            user_low, block_now, tile_rows[:, :, step_index], tile_columns[:, :, step_index],
            tile_counts[:, :, step_index], ratings[:, :, step_index]))
        user_grad = user_grad.reshape(USERS_ALL, K)
        item_grad = jnp.roll(item_grad, -step_index, axis=0).reshape(ITEMS, K)
        users_now = users_now + 0.01 * (user_grad - 0.05 * users_now)
        items_now = items_now + 0.003 * (item_grad - 0.05 * items_now)
    blocks = items_now.reshape(STRATA, ITEM_TILES * TILE, K)
    return users_now, jnp.roll(blocks, STEPS - 1, axis=0).reshape(ITEMS, K)
```

```python
import functools

import jax
import jax.numpy as jnp
from jax import lax
from jax.experimental import pallas as pl
from jax.experimental.pallas import tpu as pltpu
from jax.sharding import PartitionSpec as P

STRATA = 16
MESH = pl.DeviceIdType.MESH
F32 = jnp.float32
BF16 = jnp.bfloat16

AG = {
    "z": 0,
    "a_own": 1, "a_far": 2, "a_relay": 3,
    "b_own": 4, "b_far": 5, "b_relay": 6,
    "c0_own": 7, "c0_far": 8,
    "c1_0": 9, "c1_1": 10, "c2_0": 11, "c2_1": 12, "c3_0": 13, "c3_1": 14,
    "next": 15, "master": 16,
}
AG_COUNT = 17
RS_COUNT = 11


def kernel(
    steps, table, users_hbm, items_ref, ratings_hbm, users_out, items_out,
    rate0, rate1, uf, ub, e_ref, g_ref, s_ref, v0, v1, low_ref, master, master_in,
    rc, ry, rz, load_sem, store_sem, ag_send, ag_recv, rs_send, rs_recv,
):
    s = lax.axis_index("strata")
    u = lax.axis_index("users")
    y = u // 4
    zh = (u // 2) % 2
    c = u % 2
    ya = y + 1 - 2 * (y % 2)
    yb = 3 - y
    yo = (y + 2) % 4
    chunk_y = (y, ya, yb, yo)

    def user(yy, zz, cc):
        return yy * 4 + zz * 2 + cc

    behind = (s + STRATA - 1) % STRATA
    ahead = (s + 1) % STRATA
    core_peer = (s, user(y, zh, 1 - c))
    a_peer = (s, user(ya, zh, c))
    b_peer = (s, user(yb, zh, c))
    z_peer = (s, user(y, 1 - zh, c))
    next_peer = (ahead, u)
    next_z_peer = (ahead, user(y, 1 - zh, c))

    rates = (rate0, rate1)
    vs = (v0, v1)
    slots = ratings_hbm.shape[1]
    row_count = uf.shape[0]
    rows = ub.shape[0] // 8

    barrier = pltpu.get_barrier_semaphore()
    peers = (
        core_peer, a_peer, b_peer, z_peer, next_peer, next_z_peer,
        (behind, u), (behind, user(y, 1 - zh, c)),
    )
    for peer in peers:
        pl.semaphore_signal(barrier, inc=1, device_id=peer, device_id_type=MESH)

    load_users = pltpu.make_async_copy(users_hbm, uf, load_sem.at[0])
    load_users.start()
    load_rates = []
    for t in range(steps):
        copy = pltpu.make_async_copy(
            ratings_hbm.at[t], rates[t].at[pl.ds(0, slots)], load_sem.at[1 + t]
        )
        copy.start()
        load_rates.append(copy)
    for t in range(steps):
        rates[t][slots] = jnp.zeros(rates[t].shape[1:], jnp.int32)

    v0[y, zh, c] = items_ref[...].astype(BF16)
    pl.semaphore_wait(barrier, len(peers))

    def send(src, dst, sems, n, peer):
        copy = pltpu.make_async_remote_copy(
            src_ref=src, dst_ref=dst, send_sem=sems[0].at[n], recv_sem=sems[1].at[n],
            device_id=peer, device_id_type=MESH,
        )
        copy.start()
        return copy

    def convert_users():
        load_users.wait()

        def body(i, carry):
            at = pl.ds(pl.multiple_of(i * rows, rows), rows)
            ub[at, :] = uf[at, :].astype(BF16)
            return carry

        lax.fori_loop(0, 8, body, 0)

    def residuals(t, k):
        yy = chunk_y[k]
        width = e_ref.shape[2]

        def body(i, carry):
            at = pl.ds(pl.multiple_of(i * rows, rows), rows)
            v = vs[t][yy].reshape(width, ub.shape[1])
            p = lax.dot_general(
                ub[at, :], v, (((1,), (1,)), ((), ())), preferred_element_type=F32
            )
            tile = rates[t].shape[1]
            for r in range(rows // tile):
                for j in range(width // tile):
                    slot = table[t * 128 + (i * (rows // tile) + r) * 8 + yy * 2 + j]
                    rate = rates[t][slot]
                    part = p[r * tile:(r + 1) * tile, j * tile:(j + 1) * tile]
                    e = jnp.where(rate > 0, rate.astype(F32) - part, 0.0).astype(BF16)
                    e_ref[
                        k, pl.ds(pl.multiple_of(i * rows + r * tile, tile), tile),
                        j * tile:(j + 1) * tile,
                    ] = e
            return carry

        lax.fori_loop(0, 8, body, 0)

    def item_grad(k):
        g = lax.dot_general(
            e_ref[k], ub[...], (((0,), (0,)), ((), ())), preferred_element_type=F32
        )
        g_ref[k] = g.reshape(g_ref.shape[1:])

    def user_update(t, piece, last):
        def body(i, carry):
            at = pl.ds(pl.multiple_of((piece * 2 + i) * rows, rows), rows)
            total = None
            for k in range(4):
                v = vs[t][chunk_y[k]].reshape(e_ref.shape[2], ub.shape[1])
                term = jnp.dot(e_ref[k, at, :], v, preferred_element_type=F32)
                total = term if total is None else total + term
            now = uf[at, :]
            uf[at, :] = now + 0.01 * (total - 0.05 * now)
            return carry

        lax.fori_loop(0, 2, body, 0)
        if last:
            at = pl.ds(piece * 2 * rows, 2 * rows)
            copy = pltpu.make_async_copy(uf.at[at], users_out.at[at], store_sem.at[piece])
            copy.start()
            return copy
        return None

    def low_users(t):
        def body(i, carry):
            at = pl.ds(pl.multiple_of(i * rows, rows), rows)
            ub[at, :] = uf[at, :].astype(BF16)
            return carry

        lax.fori_loop(0, 8, body, 0)

    for t in range(steps):
        last = t == steps - 1
        v = vs[t]
        sems = (ag_send.at[t], ag_recv.at[t])
        sent = []

        def push(name, yy, zz, peer):
            copy = send(v.at[yy, zz, c], v.at[yy, zz, c], sems, AG[name], peer)
            sent.append(copy)
            return copy

        if t == 0:
            far = push("z", y, zh, z_peer)
        else:
            own_copy.wait_recv()
        a_own = push("a_own", y, zh, a_peer)
        b_own = push("b_own", y, zh, b_peer)
        c_own = push("c0_own", y, zh, core_peer)
        if t == 0:
            convert_users()
            load_rates[0].wait()
        far.wait_recv()
        a_far = push("a_far", y, 1 - zh, a_peer)
        b_far = push("b_far", y, 1 - zh, b_peer)
        c_far = push("c0_far", y, 1 - zh, core_peer)
        if t > 0:
            load_rates[t].wait()
        c_own.wait_recv()
        c_far.wait_recv()
        residuals(t, 0)
        a_own.wait_recv()
        a_far.wait_recv()
        a_relay = push("b_relay", ya, 0, b_peer)
        c1 = (push("c1_0", ya, 0, core_peer), push("c1_1", ya, 1, core_peer))
        b_own.wait_recv()
        b_far.wait_recv()
        b_relay = push("a_relay", yb, 1, a_peer)
        c2 = (push("c2_0", yb, 0, core_peer), push("c2_1", yb, 1, core_peer))
        c1[0].wait_recv()
        c1[1].wait_recv()
        residuals(t, 1)
        a_relay.wait_recv()
        c3_0 = push("c3_0", yo, 0, core_peer)
        b_relay.wait_recv()
        c3_1 = push("c3_1", yo, 1, core_peer)
        c2[0].wait_recv()
        c2[1].wait_recv()
        residuals(t, 2)
        c3_0.wait_recv()
        c3_1.wait_recv()
        residuals(t, 3)

        rsems = (rs_send.at[t], rs_recv.at[t])
        out = []

        def over_core(k):
            copy = send(g_ref.at[k, :, 1 - c], rc.at[t, k], rsems, k, core_peer)
            out.append(copy)
            return copy

        def over_y(src, n, peer):
            copy = send(src, ry.at[t, n], rsems, 4 + n, peer)
            out.append(copy)
            return copy

        def core_sum(k, copy):
            copy.wait_recv()
            for z in range(2):
                s_ref[k, z] = g_ref[k, z, c] + rc[t, k, z]

        item_grad(3)
        core3 = over_core(3)
        item_grad(1)
        core1 = over_core(1)
        core_sum(3, core3)
        y0 = over_y(s_ref.at[3, 0], 0, a_peer)
        y1 = over_y(s_ref.at[3, 1], 1, b_peer)
        item_grad(2)
        core2 = over_core(2)
        core_sum(1, core1)
        y2 = over_y(s_ref.at[1, 0], 2, a_peer)
        item_grad(0)
        core0 = over_core(0)
        core_sum(2, core2)
        y3 = over_y(s_ref.at[2, 1], 3, b_peer)
        y0.wait_recv()
        s_ref[2, 0] = s_ref[2, 0] + ry[t, 0]
        y4 = over_y(s_ref.at[2, 0], 4, b_peer)
        y1.wait_recv()
        s_ref[1, 1] = s_ref[1, 1] + ry[t, 1]
        y5 = over_y(s_ref.at[1, 1], 5, a_peer)
        core_sum(0, core0)
        stores = [user_update(t, 0, last)]
        y2.wait_recv()
        y3.wait_recv()
        y4.wait_recv()
        y5.wait_recv()
        s_ref[0, 0] = s_ref[0, 0] + ry[t, 2] + ry[t, 4]
        s_ref[0, 1] = s_ref[0, 1] + ry[t, 3] + ry[t, 5]
        over_z = send(s_ref.at[0, 1 - zh], rz.at[t], rsems, 10, z_peer)
        out.append(over_z)
        for piece in range(1, 4):
            stores.append(user_update(t, piece, last))
        if not last:
            low_users(t)
        if t > 0:
            master_copy.wait_recv()
        over_z.wait_recv()
        grad = s_ref[0, zh] + rz[t]
        now = items_ref[...] if t == 0 else master_in[...]
        now = now + 0.003 * (grad - 0.05 * now)
        if last:
            items_out[...] = now
        else:
            low_ref[...] = now.astype(BF16)
            master[...] = now
            nsems = (ag_send.at[t + 1], ag_recv.at[t + 1])
            dst = vs[t + 1].at[y, zh, c]
            far = send(low_ref, dst, nsems, AG["z"], next_z_peer)
            own_copy = send(low_ref, dst, nsems, AG["next"], next_peer)
            master_copy = send(master, master_in, nsems, AG["master"], next_peer)
            late = [far, own_copy, master_copy]
        for copy in sent + out:
            copy.wait_send()
        for copy in stores:
            if copy is not None:
                copy.wait()
        if last:
            for copy in late:
                copy.wait_send()


def shards(user_factors, item_factors, tile_rows, tile_columns, tile_counts, ratings):
    steps, slots, tile = ratings.shape[2], ratings.shape[3], ratings.shape[4]
    users, width = user_factors.shape
    own = item_factors.shape[0]
    pairs = 128
    pair = tile_rows[0, 0] * 8 + tile_columns[0, 0]
    slot = jnp.arange(slots, dtype=jnp.int32)
    live = slot[None, :] < tile_counts[0, 0][:, None]
    named = (pair[:, None, :] == jnp.arange(pairs)[None, :, None]) & live[:, None, :]
    table = slots + jnp.sum(jnp.where(named, slot - slots, 0), axis=2, dtype=jnp.int32)

    anywhere = pl.BlockSpec(memory_space=pl.ANY)
    vmem = pl.BlockSpec(memory_space=pltpu.VMEM)
    block = (4, 2, 2, own, width)
    return pl.pallas_call(
        functools.partial(kernel, steps),
        out_shape=(
            jax.ShapeDtypeStruct((users, width), F32),
            jax.ShapeDtypeStruct((own, width), F32),
        ),
        in_specs=[pl.BlockSpec(memory_space=pltpu.SMEM), anywhere, vmem, anywhere],
        out_specs=(anywhere, vmem),
        scratch_shapes=[
            pltpu.VMEM((slots + 1, tile, tile), jnp.int32),
            pltpu.VMEM((slots + 1, tile, tile), jnp.int32),
            pltpu.VMEM((users, width), F32),
            pltpu.VMEM((users, width), BF16),
            pltpu.VMEM((4, users, 4 * own), BF16),
            pltpu.VMEM(block, F32),
            pltpu.VMEM((4, 2, own, width), F32),
            pltpu.VMEM(block, BF16),
            pltpu.VMEM(block, BF16),
            pltpu.VMEM((own, width), BF16),
            pltpu.VMEM((own, width), F32),
            pltpu.VMEM((own, width), F32),
            pltpu.VMEM((steps, 4, 2, own, width), F32),
            pltpu.VMEM((steps, 6, own, width), F32),
            pltpu.VMEM((steps, own, width), F32),
            pltpu.SemaphoreType.DMA((1 + steps,)),
            pltpu.SemaphoreType.DMA((4,)),
            pltpu.SemaphoreType.DMA((steps, AG_COUNT)),
            pltpu.SemaphoreType.DMA((steps, AG_COUNT)),
            pltpu.SemaphoreType.DMA((steps, RS_COUNT)),
            pltpu.SemaphoreType.DMA((steps, RS_COUNT)),
        ],
        compiler_params=pltpu.CompilerParams(
            collective_id=0, has_side_effects=True, vmem_limit_bytes=56 << 20
        ),
        name="sgd_steps",
    )(table.reshape(-1), user_factors, item_factors, ratings[0, 0])


def solution(mesh):
    placed = (
        P(("strata", "users"), None),
        P(("strata", "users"), None),
        P("strata", "users", None, None),
        P("strata", "users", None, None),
        P("strata", "users", None),
        P("strata", "users", None, None, None, None),
    )
    return jax.shard_map(
        shards,
        mesh=mesh,
        in_specs=placed,
        out_specs=(P(("strata", "users"), None), P(("strata", "users"), None)),
        check_vma=False,
    )
```

```python
import functools

import jax
import jax.numpy as jnp
from jax import lax
from jax.experimental import pallas as pl
from jax.experimental.pallas import tpu as pltpu
from jax.sharding import PartitionSpec as P

STRATA = 16
MESH = pl.DeviceIdType.MESH
F32 = jnp.float32
BF16 = jnp.bfloat16

PAIRS = 128
LIMIT = 32766.0
STEP = 64.0
PAIRS = 128
LIMIT = 32766.0
STEP = 64.0


def encode(x):
    top = jnp.maximum(jnp.max(jnp.abs(x), axis=0, keepdims=True), 1e-30)
    level = jnp.ceil(jnp.log2(top) * STEP)
    code = jnp.round(x * (LIMIT * jnp.exp2(level * (-1.0 / STEP)))).astype(jnp.int32)
    level = jnp.broadcast_to(level.astype(jnp.int32), (16, x.shape[1]))
    return code.astype(jnp.int16), level.astype(jnp.int16)


def decode(ref):
    rows = ref.shape[0] - 16
    level = ref[rows:, :].astype(jnp.int32)[0:1, :].astype(F32)
    scale = jnp.exp2(level * (1.0 / STEP)) * (1.0 / LIMIT)
    return ref[:rows, :].astype(jnp.int32).astype(F32) * scale


def kernel(
    steps, rows_ref, columns_ref, counts_ref, users_hbm, items_ref, ratings_hbm,
    uf, items_out,
    rate0, rate1, ub, e_ref, g_ref, s_ref, v0, v1, master,
    rc, code_out, code_in, shift_out, shift_in, last_out, last_in,
    table_v, table, load_sem, ag_send, ag_recv, rs_send, rs_recv, next_send, next_recv,
):
    s = lax.axis_index("strata")
    u = lax.axis_index("users")
    y = u // 4
    zh = (u // 2) % 2
    c = u % 2
    ya = y + 1 - 2 * (y % 2)
    yb = 3 - y
    yo = (y + 2) % 4
    chunk_y = (y, ya, yb, yo)

    def user(yy, zz, cc):
        return yy * 4 + zz * 2 + cc

    behind = (s + STRATA - 1) % STRATA
    ahead = (s + 1) % STRATA
    y_peers = tuple((s, user(yy, zh, c)) for yy in chunk_y)
    core_peer = (s, user(y, zh, 1 - c))
    z_peer = (s, user(y, 1 - zh, c))
    next_peers = ((ahead, u), (ahead, user(y, 1 - zh, c)))
    peers = (
        core_peer, z_peer, *y_peers[1:], *next_peers,
        (behind, u), (behind, user(y, 1 - zh, c)),
    )

    rates = (rate0, rate1)
    vs = (v0, v1)
    slots, tile = ratings_hbm.shape[1], ratings_hbm.shape[2]
    user_count, width = ub.shape
    own = items_ref.shape[0]
    wide = 4 * own

    barrier = pltpu.get_barrier_semaphore()
    for peer in peers:
        pl.semaphore_signal(barrier, inc=1, device_id=peer, device_id_type=MESH)

    load_users = pltpu.make_async_copy(users_hbm, uf, load_sem.at[0])
    load_users.start()
    load_rates = []
    for t in range(steps):
        copy = pltpu.make_async_copy(
            ratings_hbm.at[t], rates[t].at[pl.ds(0, slots)], load_sem.at[1 + t]
        )
        copy.start()
        load_rates.append(copy)
    for t in range(steps):
        rates[t][slots] = jnp.zeros((tile, tile), jnp.int32)
    v0[y, zh, c] = items_ref[...].astype(BF16)

    def send(src, dst, sems, n, peer):
        copy = pltpu.make_async_remote_copy(
            src_ref=src, dst_ref=dst, send_sem=sems[0].at[n], recv_sem=sems[1].at[n],
            device_id=peer, device_id_type=MESH,
        )
        copy.start()
        return copy

    def low_users(i, carry):
        at = pl.ds(pl.multiple_of(i * 256, 256), 256)
        ub[at, :] = uf[at, :].astype(BF16)
        return carry

    def fill_table():
        lanes = lax.broadcasted_iota(jnp.int32, (1, PAIRS), 1)
        for t in range(steps):
            count = counts_ref[0, 0, t]

            def name(m, found):
                pair = rows_ref[0, 0, t, m] * 8 + columns_ref[0, 0, t, m]
                pair = jnp.where(m < count, pair, -1)
                return jnp.where(lanes == pair, m, found)

            table_v[t:t + 1, :] = lax.fori_loop(
                0, slots, name, jnp.full((1, PAIRS), slots, jnp.int32)
            )
        copy = pltpu.make_async_copy(table_v, table, load_sem.at[1 + steps])
        copy.start()
        copy.wait()

    def residuals(t, k):
        yy = chunk_y[k]
        p = lax.dot_general(
            ub[...], vs[t][yy].reshape(wide, width), (((1,), (1,)), ((), ())),
            preferred_element_type=F32,
        )
        for r in range(user_count // tile):
            for j in range(wide // tile):
                rate = rates[t][table[t, r * 8 + yy * 2 + j]]
                part = p[r * tile:(r + 1) * tile, j * tile:(j + 1) * tile]
                e = jnp.where(rate > 0, rate.astype(F32) - part, 0.0).astype(BF16)
                e_ref[k, r * tile:(r + 1) * tile, j * tile:(j + 1) * tile] = e

    def item_grad(k):
        g = lax.dot_general(
            e_ref[k], ub[...], (((0,), (0,)), ((), ())), preferred_element_type=F32
        )
        g_ref[k] = g.reshape(g_ref.shape[1:])

    def user_update(t, piece):
        at = pl.ds(piece * (user_count // 4), user_count // 4)
        total = None
        for k in range(4):
            v = vs[t][chunk_y[k]].reshape(wide, width)
            term = jnp.dot(e_ref[k, at, :], v, preferred_element_type=F32)
            total = term if total is None else total + term
        now = uf[at, :]
        uf[at, :] = now + 0.01 * (total - 0.05 * now)

    pl.semaphore_wait(barrier, len(peers))

    for t in range(steps):
        last = t == steps - 1
        v = vs[t]
        sems = (ag_send.at[t], ag_recv.at[t])
        sent = []

        def push(part, n, peer):
            copy = send(part, part, sems, n, peer)
            sent.append(copy)
            return copy

        if t == 0:
            far = push(v.at[y, zh, c], 0, z_peer)
            near = [push(v.at[y, zh, c], k, y_peers[k]) for k in (3, 1, 2)]
            core = [push(v.at[y, zh, c], 4, core_peer)]
            load_users.wait()
            lax.fori_loop(0, user_count // 256, low_users, 0)
            fill_table()
            far.wait_recv()
            more = [push(v.at[y, 1 - zh, c], 5 + k, y_peers[k]) for k in (3, 1, 2)]
            core.append(push(v.at[y, 1 - zh, c], 5, core_peer))
            arrivals = {k: [near[i], more[i]] for i, k in enumerate((3, 1, 2))}
        else:
            both = v.at[y, :, c]
            near = [push(both, k, y_peers[k]) for k in (3, 1, 2)]
            core = [push(both, 4, core_peer)]
            arrivals = {k: [near[i]] for i, k in enumerate((3, 1, 2))}
        load_rates[t].wait()
        for copy in core:
            copy.wait_recv()
        residuals(t, 0)
        forward = {}
        for k in (1, 2, 3):
            for copy in arrivals[k]:
                copy.wait_recv()
            forward[k] = push(v.at[chunk_y[k], :, c], 8 + k, core_peer)
            if k > 1:
                forward[k - 1].wait_recv()
                residuals(t, k - 1)
        if t == 0:
            carried = [
                send(items_ref, master.at[zh], (next_send, next_recv), i, next_peers[i])
                for i in range(2)
            ]
        forward[3].wait_recv()
        residuals(t, 3)

        rsems = (rs_send.at[t], rs_recv.at[t])

        def over_core(k):
            item_grad(k)
            copy = send(g_ref.at[k, :, 1 - c], rc.at[t, k], rsems, k, core_peer)
            sent.append(copy)
            return copy

        def core_sum(k, copy):
            copy.wait_recv()
            return (g_ref[k, :, c] + rc[t, k]).reshape(2 * own, width)

        def over_y(k, copy):
            code, level = encode(core_sum(k, copy))
            code_out[t, k - 1, :2 * own] = code
            code_out[t, k - 1, 2 * own:] = level
            copy = send(
                code_out.at[t, k - 1], code_in.at[t, k - 1], rsems, 3 + k, y_peers[k]
            )
            sent.append(copy)
            return copy

        core3 = over_core(3)
        core1 = over_core(1)
        y3 = over_y(3, core3)
        core2 = over_core(2)
        y1 = over_y(1, core1)
        core0 = over_core(0)
        y2 = over_y(2, core2)
        user_update(t, 0)
        s_ref[...] = core_sum(0, core0)
        user_update(t, 1)
        for k, copy in ((3, y3), (1, y1), (2, y2)):
            copy.wait_recv()
            s_ref[...] = s_ref[...] + decode(code_in.at[t, k - 1])
        if not last:
            code, level = encode(s_ref[...])
            shift_out[:2 * own] = code
            shift_out[2 * own:] = level
            shifted = [
                send(shift_out, shift_in.at[zh], (next_send, next_recv), 2 + i, next_peers[i])
                for i in range(2)
            ]
            user_update(t, 2)
            user_update(t, 3)
            lax.fori_loop(0, user_count // 256, low_users, 0)
            for copy in carried + shifted:
                copy.wait_recv()
            grad = decode(shift_in.at[0]) + decode(shift_in.at[1])
            now = master[...].reshape(2 * own, width)
            now = now + 0.003 * (grad - 0.05 * now)
            master[...] = now.reshape(2, own, width)
            vs[t + 1][y, :, c] = now.astype(BF16).reshape(2, own, width)
        else:
            code, level = encode(s_ref[pl.ds(pl.multiple_of((1 - zh) * own, own), own), :])
            last_out[:own] = code
            last_out[own:] = level
            final = send(last_out, last_in, rsems, 7, z_peer)
            sent.append(final)
            user_update(t, 2)
            user_update(t, 3)
            now = master[zh]
            kept = s_ref[pl.ds(pl.multiple_of(zh * own, own), own), :]
            final.wait_recv()
            grad = kept + decode(last_in)
            items_out[...] = now + 0.003 * (grad - 0.05 * now)
        for copy in sent:
            copy.wait_send()
    for copy in carried + shifted:
        copy.wait_send()


def shards(user_factors, item_factors, tile_rows, tile_columns, tile_counts, ratings):
    steps, slots, tile = ratings.shape[2], ratings.shape[3], ratings.shape[4]
    users, width = user_factors.shape
    own = item_factors.shape[0]
    anywhere = pl.BlockSpec(memory_space=pl.ANY)
    vmem = pl.BlockSpec(memory_space=pltpu.VMEM)
    smem = pl.BlockSpec(memory_space=pltpu.SMEM)
    block = (4, 2, 2, own, width)
    coded = 2 * own + 16
    return pl.pallas_call(
        functools.partial(kernel, steps),
        out_shape=(
            pltpu.VMEM((users, width), F32),
            pltpu.VMEM((own, width), F32),
        ),
        in_specs=[smem, smem, smem, anywhere, vmem, anywhere],
        out_specs=(vmem, vmem),
        scratch_shapes=[
            pltpu.VMEM((slots + 1, tile, tile), jnp.int32),
            pltpu.VMEM((slots + 1, tile, tile), jnp.int32),
            pltpu.VMEM((users, width), BF16),
            pltpu.VMEM((4, users, 4 * own), BF16),
            pltpu.VMEM(block, F32),
            pltpu.VMEM((2 * own, width), F32),
            pltpu.VMEM(block, BF16),
            pltpu.VMEM(block, BF16),
            pltpu.VMEM((2, own, width), F32),
            pltpu.VMEM((steps, 4, 2, own, width), F32),
            pltpu.VMEM((steps, 3, coded, width), jnp.int16),
            pltpu.VMEM((steps, 3, coded, width), jnp.int16),
            pltpu.VMEM((coded, width), jnp.int16),
            pltpu.VMEM((2, coded, width), jnp.int16),
            pltpu.VMEM((own + 16, width), jnp.int16),
            pltpu.VMEM((own + 16, width), jnp.int16),
            pltpu.VMEM((steps, PAIRS), jnp.int32),
            pltpu.SMEM((steps, PAIRS), jnp.int32),
            pltpu.SemaphoreType.DMA((2 + steps,)),
            pltpu.SemaphoreType.DMA((steps, 12)),
            pltpu.SemaphoreType.DMA((steps, 12)),
            pltpu.SemaphoreType.DMA((steps, 8)),
            pltpu.SemaphoreType.DMA((steps, 8)),
            pltpu.SemaphoreType.DMA((4,)),
            pltpu.SemaphoreType.DMA((4,)),
        ],
        compiler_params=pltpu.CompilerParams(
            collective_id=0, has_side_effects=True, vmem_limit_bytes=56 << 20
        ),
        name="sgd_steps",
    )(tile_rows, tile_columns, tile_counts, user_factors, item_factors, ratings[0, 0])


def solution(mesh):
    placed = (
        P(("strata", "users"), None),
        P(("strata", "users"), None),
        P("strata", "users", None, None),
        P("strata", "users", None, None),
        P("strata", "users", None),
        P("strata", "users", None, None, None, None),
    )
    return jax.shard_map(
        shards,
        mesh=mesh,
        in_specs=placed,
        out_specs=(P(("strata", "users"), None), P(("strata", "users"), None)),
        check_vma=False,
    )
```
